32 devices in a mesh: groups: 1, blk: 16 (over z, y, x), heads: 2 (over core).
Axes of the slice: x: 2, y: 2, z: 4, core: 2. Of those that a mesh axis runs over, the one named last changes fastest.
Arguments:
- queries: bfloat16 [4096, 2048], P(('groups', 'blk', 'heads')), may hold values from -186 to 186
- keys: bfloat16 [4096, 1024], P(('groups', 'blk', 'heads')), may hold values from -6 to 6
- values: bfloat16 [4096, 1024], P(('groups', 'blk', 'heads')), may hold values from -6 to 6
- upstream: bfloat16 [4096, 2048], P(('groups', 'blk', 'heads')), may hold values from -6 to 6
- doc_ids: int32 [32], P('groups'), may hold values from 0 to 3, never falling along the last dimension, each value on 1 to 16 neighbouring positions
- band: int32 [32], P('groups'), may hold values from 0 to 8, as said below
Outputs:
- query_grad: bfloat16 [4096, 2048], P(('groups', 'blk', 'heads'))
- key_gradient: bfloat16 [4096, 1024], P(('groups', 'blk', 'heads'))
- value_gradient: bfloat16 [4096, 1024], P(('groups', 'blk', 'heads'))
The draws below stay inside these ranges and needn't reach their ends.
Inputs may be any that keep to these rules, and one draw needn't show every extreme that they name: `band`: earlier blocks a query block may see; some block sees 8 and some sees 0.
All inputs are finite; a program needn't handle non-finite values.
Results may differ from the reference program's by a relative error of at most 0.0083.
Values may be sent and summed in bfloat16 or wider, within the bound.
A program may use at most 64 MiB of HBM per device.

```python
import math
import jax
import jax.numpy as jnp
import numpy as np
from jax import lax

QUERY_HEADS = 16
KEY_VALUE_HEADS = 8
HEAD_SIZE = 128
SCALAR = 168
WINDOW_TOKENS = 1024
MASK_BLOCK = 128
SEQUENCE_TOKENS = 4096
NB = 32
WB = 8
DOCS = 4
DOC_MOST = 16


def common_draw(key):
    base_offset = jnp.clip(jax.random.normal(jax.random.fold_in(key, 11), (SEQUENCE_TOKENS, KEY_VALUE_HEADS, HEAD_SIZE), jnp.float32), -6.0, 6.0)
    levels = jax.random.randint(jax.random.fold_in(key, 13), (SEQUENCE_TOKENS,), 0, 3)
    position = jnp.arange(SEQUENCE_TOKENS)
    chosen = position < 0
    strength = jnp.where(chosen, 10.0 + 10.0 * levels.astype(jnp.float32), 0.0)
    return (base_offset, strength)


def draw_keys(key, part):
    base_offset, strength = common_draw(key)
    after = jnp.roll(strength, -1)
    following = jnp.roll(base_offset, -1, axis=0)
    shrink = 1.0 - 0.2 / jnp.maximum(after, 1.0)
    mixed_rows = jnp.where((after > 0.0)[:, None, None], shrink[:, None, None] * following, base_offset)
    return mixed_rows.reshape(SEQUENCE_TOKENS, KEY_VALUE_HEADS * HEAD_SIZE).astype(jnp.bfloat16)


def draw_queries(key, part):
    base_offset, strength = common_draw(key)
    noise = jnp.clip(jax.random.normal(jax.random.fold_in(key, 14), (SEQUENCE_TOKENS, QUERY_HEADS, HEAD_SIZE), jnp.float32), -6.0, 6.0)
    block_aligned = jnp.repeat(base_offset, QUERY_HEADS // KEY_VALUE_HEADS, axis=1)
    mixed_rows = noise + strength[:, None, None] * block_aligned
    return mixed_rows.reshape(SEQUENCE_TOKENS, QUERY_HEADS * HEAD_SIZE).astype(jnp.bfloat16)


def draw_band(key, part):
    widths = jax.random.randint(jax.random.fold_in(key, 21), (NB,), 0, WB + 1)
    widest = jax.random.randint(jax.random.fold_in(key, 22), (), 0, NB)
    narrow = jax.random.randint(jax.random.fold_in(key, 23), (), 0, NB)
    position = jnp.arange(NB)
    widths = jnp.where(position == narrow, 0, widths)
    widths = jnp.where(position == widest, WB, widths)
    return widths.astype(jnp.int32)


def block_levels(rng, shape, cuts, least, largest):
    loudness = 1.0
    for dim, parts in cuts:
        steps = jax.random.uniform(jax.random.fold_in(jax.random.fold_in(rng, 6), dim), (parts,), jnp.float32, least / len(cuts), largest / len(cuts))
        loudness = loudness * jnp.repeat(jnp.exp(steps), shape[dim] // parts).reshape((-1,) + (1,) * (len(shape) - 1 - dim))
    return loudness


def split_up(amount, total, bound, slope):
    portions = [(1 << 20) // math.isqrt(standing ** slope) + 1 for standing in range(2, amount + 1)]
    spare, given = total - bound - (amount - 1), [1] * (amount - 1)
    while spare > 0:
        movable = [i for i in range(amount - 1) if given[i] < bound]
        pool, left = sum([portions[i] for i in movable]), spare
        for i in movable:
            more = min(bound - given[i], max(1, left * portions[i] // pool), spare)
            given[i] = given[i] + more
            spare = spare - more
    return np.array([bound] + given)


def uneven(key, number_of, total, bound, slope):
    if number_of == 2:
        one = jax.random.randint(key, (), max(1, total - bound), min(bound, total - 1) + 1)
        return jnp.stack([one, total - one])
    sizes = jnp.asarray(split_up(number_of, total, bound, slope), jnp.int32)
    pairs = (number_of - 1) // 2
    donor, sink = sizes[1:1 + 2 * pairs:2], sizes[2:2 + 2 * pairs:2]
    slack = jnp.minimum(donor - 1, bound - sink)
    moved = jax.random.randint(jax.random.fold_in(key, 1), (pairs,), 0, 1 << 20) % (slack + 1)
    sizes = sizes.at[1:1 + 2 * pairs:2].set(donor - moved).at[2:2 + 2 * pairs:2].set(sink + moved)
    return sizes[jax.random.permutation(jax.random.fold_in(key, 2), number_of)]


def scatter_about(own_key, dims, width, most, cuts=(), kind=jnp.bfloat16):
    values = jax.random.normal(own_key, dims, jnp.float32) * width
    if len(cuts) > 0:
        values = block_levels(own_key, dims, cuts, -0.22, 0.18) * values
    return jnp.clip(values, min=-most, max=most).astype(kind)


def setup_inputs(seed: int = 0, part: int = 0) -> dict:
    streams_of = jax.random.split(jax.random.key(seed), 7)
    own_keys = jax.random.split(jax.random.fold_in(streams_of[6], part), 7)
    queries = draw_queries(jax.random.fold_in(jax.random.fold_in(streams_of[6], part), 71), part)
    keys = draw_keys(jax.random.fold_in(jax.random.fold_in(streams_of[6], part), 71), part)
    values = scatter_about(own_keys[2], (SEQUENCE_TOKENS, KEY_VALUE_HEADS * HEAD_SIZE), 1.0, 6.0, ((0, 32),))
    upstream = scatter_about(own_keys[3], (SEQUENCE_TOKENS, QUERY_HEADS * HEAD_SIZE), 1.0, 6.0, ((0, 32),))
    doc_ids = jnp.searchsorted(jnp.cumsum(uneven(own_keys[4], DOCS, NB, DOC_MOST, 1)), jnp.arange(NB), side="right").astype(jnp.int32)
    band = draw_band(jax.random.fold_in(jax.random.fold_in(streams_of[6], part), 71), part)
    return {"queries": queries, "keys": keys, "values": values, "upstream": upstream, "doc_ids": doc_ids, "band": band}


def reference(queries, keys, values, upstream, doc_ids, band):
    blocks = SEQUENCE_TOKENS // MASK_BLOCK
    window_blocks = WINDOW_TOKENS // MASK_BLOCK
    group_ratio = QUERY_HEADS // KEY_VALUE_HEADS
    scale = SCALAR ** -0.5
    span_extent = WINDOW_TOKENS + MASK_BLOCK
    leading_rows = jnp.zeros((WINDOW_TOKENS, KEY_VALUE_HEADS * HEAD_SIZE), jnp.bfloat16)
    key_padding = jnp.concatenate([leading_rows, keys], 0)
    value_padding = jnp.concatenate([leading_rows, values], 0)
    doc_pad = jnp.concatenate([jnp.full((window_blocks,), -1, jnp.int32), doc_ids.astype(jnp.int32)])
    offsets = jnp.arange(window_blocks + 1, dtype=jnp.int32)
    causal = jnp.arange(span_extent, dtype=jnp.int32)[None, :] <= jnp.arange(MASK_BLOCK, dtype=jnp.int32)[:, None] + WINDOW_TOKENS

    def one_block(carry, index):
        key_accumulator, value_accumulator = carry
        start_index = (index * MASK_BLOCK).astype(jnp.int32)
        query_row_slice = lax.dynamic_slice_in_dim(queries, start_index, MASK_BLOCK, 0).reshape(MASK_BLOCK, KEY_VALUE_HEADS, group_ratio, HEAD_SIZE).astype(jnp.float32)
        gradient_rows = lax.dynamic_slice_in_dim(upstream, start_index, MASK_BLOCK, 0).reshape(MASK_BLOCK, KEY_VALUE_HEADS, group_ratio, HEAD_SIZE).astype(jnp.float32)
        key_row_slice = lax.dynamic_slice_in_dim(key_padding, start_index, span_extent, 0).reshape(span_extent, KEY_VALUE_HEADS, HEAD_SIZE).astype(jnp.float32)
        value_row_slice = lax.dynamic_slice_in_dim(value_padding, start_index, span_extent, 0).reshape(span_extent, KEY_VALUE_HEADS, HEAD_SIZE).astype(jnp.float32)
        key_docs = lax.dynamic_slice_in_dim(doc_pad, index.astype(jnp.int32), window_blocks + 1, 0)
        own_doc = lax.dynamic_slice_in_dim(doc_ids.astype(jnp.int32), index.astype(jnp.int32), 1, 0)
        own_band = lax.dynamic_slice_in_dim(band.astype(jnp.int32), index.astype(jnp.int32), 1, 0)
        block_ok = (key_docs == own_doc) & (window_blocks - offsets <= own_band)
        allowed = jnp.repeat(block_ok, MASK_BLOCK, total_repeat_length=span_extent)[None, :] & causal
        scores = jnp.einsum('qhrd,khd->hrqk', query_row_slice, key_row_slice) * scale
        scores = jnp.where(allowed, scores, -jnp.inf)
        top = jnp.max(scores, axis=-1, keepdims=True)
        expo = jnp.exp(scores - top)
        probs = expo / jnp.sum(expo, axis=-1, keepdims=True)
        probs_f = lax.optimization_barrier(probs.astype(jnp.bfloat16)).astype(jnp.float32)
        output = jnp.einsum('hrqk,khd->hrqd', probs_f, value_row_slice)
        delta = jnp.sum(jnp.transpose(gradient_rows, (1, 2, 0, 3)) * output, axis=-1)
        dprob = jnp.einsum('qhrd,khd->hrqk', gradient_rows, value_row_slice)
        dscore = lax.optimization_barrier((probs * (dprob - delta[..., None])).astype(jnp.bfloat16)).astype(jnp.float32)
        query_grad = jnp.einsum('hrqk,khd->qhrd', dscore, key_row_slice) * scale
        key_gradient = jnp.einsum('hrqk,qhrd->khd', dscore, query_row_slice) * scale
        value_gradient = jnp.einsum('hrqk,qhrd->khd', probs_f, gradient_rows)
        key_accumulator = lax.dynamic_update_slice_in_dim(key_accumulator, lax.dynamic_slice_in_dim(key_accumulator, start_index, span_extent, 0) + key_gradient, start_index, 0)
        value_accumulator = lax.dynamic_update_slice_in_dim(value_accumulator, lax.dynamic_slice_in_dim(value_accumulator, start_index, span_extent, 0) + value_gradient, start_index, 0)
        return (key_accumulator, value_accumulator), query_grad.reshape(MASK_BLOCK, QUERY_HEADS * HEAD_SIZE).astype(jnp.bfloat16)

    empty_rows = jnp.zeros((WINDOW_TOKENS + SEQUENCE_TOKENS, KEY_VALUE_HEADS, HEAD_SIZE), jnp.float32)
    (key_accumulator, value_accumulator), query_parts = lax.scan(one_block, (empty_rows, empty_rows), jnp.arange(blocks, dtype=jnp.int32))
    query_grad = query_parts.reshape(SEQUENCE_TOKENS, QUERY_HEADS * HEAD_SIZE)
    key_gradient = key_accumulator[WINDOW_TOKENS:].reshape(SEQUENCE_TOKENS, KEY_VALUE_HEADS * HEAD_SIZE).astype(jnp.bfloat16)
    value_gradient = value_accumulator[WINDOW_TOKENS:].reshape(SEQUENCE_TOKENS, KEY_VALUE_HEADS * HEAD_SIZE).astype(jnp.bfloat16)
    return (query_grad, key_gradient, value_gradient)
```

```python
import functools
import math

import jax
import jax.numpy as jnp
from jax import lax
from jax.experimental import pallas as pl
from jax.experimental.pallas import tpu as pltpu
from jax.sharding import PartitionSpec as P

HEAD = 128
SCALE = 168 ** -0.5
LOG2E = math.log2(math.e)
WINDOW = 1024
BLOCK = 128
WB = WINDOW // BLOCK
GROUP = 2
QW = GROUP * HEAD
MESH = pl.DeviceIdType.MESH
HIDDEN = -1e30
SPAN = WINDOW + BLOCK
NT = (((1,), (1,)), ((), ()))
TN = (((0,), (0,)), ((), ()))


def place(cores):
    chips = WB // cores
    blk, core = lax.axis_index("blk"), lax.axis_index("heads")
    return blk // chips, (blk % chips) * cores + core


def device_of(cores, plane, local):
    return {"blk": plane * (WB // cores) + local // cores, "heads": local % cores}


def greet(cores, planes, plane, me):
    barrier = pltpu.get_barrier_semaphore()

    def signal(where):
        pl.semaphore_signal(barrier, inc=1, device_id=where, device_id_type=MESH)

    for r in range(1, WB):
        signal(device_of(cores, plane, (me + r) % WB))

    @pl.when(plane > 0)
    def _():
        signal(device_of(cores, plane - 1, me))

    @pl.when(plane < planes - 1)
    def _():
        signal(device_of(cores, plane + 1, me))

    peers = WB - 1 + jnp.minimum(plane, 1) + jnp.minimum(planes - 1 - plane, 1)
    pl.semaphore_wait(barrier, peers)


def cols(index, width):
    return pl.ds(pl.multiple_of(index * width, width), width)


def rows(index, base=0):
    return pl.ds(pl.multiple_of(base + index * BLOCK, BLOCK), BLOCK)


def stack(x):
    return jnp.concatenate([x[:, :HEAD], x[:, HEAD:]], axis=0)


def score_terms(q, g, kb, vb):
    s = lax.dot_general(kb, q, NT, preferred_element_type=jnp.float32)
    dp = lax.dot_general(vb, g, NT, preferred_element_type=jnp.float32)
    return s, dp


def soft_terms(s, dp, seen):
    tiles = []
    for i in range(WB + 1):
        tile = s[i * BLOCK : (i + 1) * BLOCK]
        if i < WB:
            tile = jnp.where(WB + 1 - i <= seen, tile, HIDDEN)
        else:
            kpos = lax.broadcasted_iota(jnp.int32, tile.shape, 0)
            qpos = lax.broadcasted_iota(jnp.int32, tile.shape, 1) % BLOCK
            tile = jnp.where(kpos <= qpos, tile, HIDDEN)
        tiles.append(tile)
    s = jnp.concatenate(tiles, axis=0)
    top = jnp.max(s, axis=0, keepdims=True)
    e = jnp.exp2((s - top) * (SCALE * LOG2E))
    inverse = 1.0 / jnp.sum(e, axis=0, keepdims=True)
    delta = jnp.sum(e * dp, axis=0, keepdims=True) * inverse
    p = e * inverse
    return p.astype(jnp.bfloat16), (p * (dp - delta)).astype(jnp.bfloat16)


def grad_terms(pb, ds, q, g, kb):
    dv = jnp.dot(pb, g, preferred_element_type=jnp.float32)
    dk = jnp.dot(ds, q, preferred_element_type=jnp.float32)
    dq = lax.dot_general(kb, ds, TN, preferred_element_type=jnp.float32)
    dq = (dq * SCALE).T.astype(jnp.bfloat16)
    return jnp.concatenate([dq[:BLOCK], dq[BLOCK:]], axis=1), dk, dv


def window_kernel(
    cores, planes, docs, band, q, k, v, g, oq, ok, ov,
    qh, gh, kw, vw, dk, dv, dq, part_k, part_v, back_k, back_v, sum_k, sum_v,
    gsend, grecv, zsend, zrecv, bsend, brecv, qsend, qrecv, rsend, rrecv,
):
    plane, me = place(cores)
    odd = (me // cores) % 2
    first, last = plane == 0, plane == planes - 1
    sources = ((k, kw, HEAD, WINDOW), (v, vw, HEAD, WINDOW), (q, qh, QW, 0), (g, gh, QW, 0))
    partial = ((dk, part_k, back_k, sum_k, ok), (dv, part_v, back_v, sum_v, ov))

    def remote(src, dst, send, recv, where):
        return pltpu.make_async_remote_copy(
            src_ref=src, dst_ref=dst, send_sem=send, recv_sem=recv,
            device_id=where, device_id_type=MESH,
        )

    def landed(ref, sem):
        pltpu.make_async_copy(ref, ref, sem).wait()

    def exchange(n, to):
        src, dst, w, base = sources[n]
        return remote(
            src.at[:, cols(to, w)], dst.at[rows(me, base), :], gsend.at[n, to], grecv.at[n, me],
            device_of(cores, plane, to),
        )

    def forward(n, of):
        dst = sources[n][1]
        return remote(
            dst.at[rows(of, WINDOW), :], dst.at[rows(of), :], zsend.at[n, of], zrecv.at[n, of],
            device_of(cores, plane + 1, me),
        )

    def backward(n, of):
        _, part, back, _, _ = partial[n]
        return remote(
            part.at[rows(of), :], back.at[rows(of), :], bsend.at[n, of], brecv.at[n, of],
            device_of(cores, plane - 1, me),
        )

    def give(src, out, w, to, send, recv):
        source, target = src.at[rows(to), :], out.at[:, cols(me, w)]

        @pl.when(to != me)
        def _():
            remote(source, target, send, recv, device_of(cores, plane, to)).start()

        @pl.when(to == me)
        def _():
            pltpu.make_async_copy(source, target, recv).start()

    def turn(i):
        return i + odd * (2 - 4 * ((i // 2) % 2))

    for n, (src, dst, w, base) in enumerate(sources):
        own = pltpu.make_async_copy(src.at[:, cols(me, w)], dst.at[rows(me, base), :], grecv.at[n, me])
        own.start()
    greet(cores, planes, plane, me)
    order = (3, 5, 4, 2, 6, 1, 7)
    for n in (0, 1):
        for r in order:
            exchange(n, (me + r) % WB).start()
    for r in order:
        for n in (2, 3):
            exchange(n, (me + r) % WB).start()

    dk[...] = jnp.zeros_like(dk)
    dv[...] = jnp.zeros_like(dv)

    @pl.when(first)
    def _():
        kw[pl.ds(0, WINDOW), :] = jnp.zeros((WINDOW, HEAD), kw.dtype)
        vw[pl.ds(0, WINDOW), :] = jnp.zeros((WINDOW, HEAD), vw.dtype)

    for n in (0, 1):
        for r in (0, 1, 7, 2, 6, 4, 3, 5):
            of = (me + r) % WB
            landed(sources[n][1].at[rows(of, WINDOW), :], grecv.at[n, of])

            @pl.when(jnp.logical_not(last))
            def _():
                forward(n, of).start()

    @pl.when(jnp.logical_not(first))
    def _():
        for n in (0, 1):

            @pl.loop(0, WB)
            def _(of):
                landed(sources[n][1].at[rows(of), :], zrecv.at[n, of])

    def send_back(j):
        @pl.when(jnp.logical_not(first))
        def _():
            part_k[rows(j), :] = (dk[rows(j), :] * SCALE).astype(jnp.bfloat16)
            part_v[rows(j), :] = dv[rows(j), :].astype(jnp.bfloat16)
            backward(0, j).start()
            backward(1, j).start()

    def seen_by(t):
        block = plane * WB + t
        seen = jnp.int32(0)
        for d in range(WB + 1):
            at = jnp.maximum(block - d, 0)
            visible = (d <= band[block]) & (block >= d) & (docs[at] == docs[block])
            seen = seen + visible.astype(jnp.int32)
        return seen

    def load(t):
        span = pl.ds(pl.multiple_of(t * BLOCK, BLOCK), SPAN)
        return stack(qh[rows(t), :]), stack(gh[rows(t), :]), kw[span, :], vw[span, :]

    def store(t, out, key_term, value_term):
        span = pl.ds(pl.multiple_of(t * BLOCK, BLOCK), SPAN)
        dk[span, :] += key_term
        dv[span, :] += value_term
        dq[rows(t), :] = out

    @pl.loop(0, WB // 2)
    def _(i):
        one = turn(2 * i)
        two = one + 1
        for t in (one, two):
            landed(qh.at[rows(t), :], grecv.at[2, t])
            landed(gh.at[rows(t), :], grecv.at[3, t])
        seen_one, seen_two = seen_by(one), seen_by(two)
        q1, g1, k1, v1 = load(one)
        q2, g2, k2, v2 = load(two)
        s1, dp1 = score_terms(q1, g1, k1, v1)
        s2, dp2 = score_terms(q2, g2, k2, v2)
        pb1, ds1 = soft_terms(s1, dp1, seen_one)
        store(one, *grad_terms(pb1, ds1, q1, g1, k1))
        pb2, ds2 = soft_terms(s2, dp2, seen_two)
        store(two, *grad_terms(pb2, ds2, q2, g2, k2))

        @pl.when(odd == 0)
        def _():
            send_back(one)
            send_back(two)

        @pl.when((odd == 1) & (i % 2 == 1))
        def _():
            for back in (2, 3, 0, 1):
                send_back(2 * i - 2 + back)

        for t in (one, two):
            give(dq, oq, QW, t, qsend.at[t], qrecv.at[me])

    @pl.loop(0, WB)
    def _(i):
        j = turn(i)
        for n in (0, 1):
            acc, _, back, total, out = partial[n]
            factor = SCALE if n == 0 else 1.0

            @pl.when(jnp.logical_not(last))
            def _():
                landed(back.at[rows(j), :], brecv.at[n, j])
                both = acc[rows(j, WINDOW), :] * factor + back[rows(j), :].astype(jnp.float32)
                total[rows(j), :] = both.astype(jnp.bfloat16)

            @pl.when(last)
            def _():
                total[rows(j), :] = (acc[rows(j, WINDOW), :] * factor).astype(jnp.bfloat16)

        for n in (0, 1):
            _, _, _, total, out = partial[n]
            give(total, out, HEAD, j, rsend.at[n, j], rrecv.at[n, me])

    @pl.loop(0, WB)
    def _(s):
        landed(oq.at[:, cols(s, QW)], qrecv.at[s])
        landed(ok.at[:, cols(s, HEAD)], rrecv.at[0, s])
        landed(ov.at[:, cols(s, HEAD)], rrecv.at[1, s])

        @pl.when(s != me)
        def _():
            for n in range(4):
                exchange(n, s).wait_send()
            where = device_of(cores, plane, s)
            remote(dq.at[rows(s), :], oq.at[:, cols(me, QW)], qsend.at[s], qrecv.at[me], where).wait_send()
            for n in (0, 1):
                _, _, _, total, out = partial[n]
                remote(
                    total.at[rows(s), :], out.at[:, cols(me, HEAD)], rsend.at[n, s], rrecv.at[n, me], where
                ).wait_send()

        for n in (0, 1):

            @pl.when(jnp.logical_not(last))
            def _():
                forward(n, s).wait_send()

            @pl.when(jnp.logical_not(first))
            def _():
                backward(n, s).wait_send()


def window_attention(cores, planes, docs, band, queries, keys, values, upstream):
    hbm = pl.BlockSpec(memory_space=pl.ANY)
    smem = pl.BlockSpec(memory_space=pltpu.SMEM)
    bf16, f32 = jnp.bfloat16, jnp.float32
    dma = pltpu.SemaphoreType.DMA
    return pl.pallas_call(
        functools.partial(window_kernel, cores, planes),
        out_shape=tuple(pltpu.VMEM(a.shape, bf16) for a in (queries, keys, values)),
        in_specs=[smem] * 2 + [hbm] * 4,
        out_specs=(pl.BlockSpec(memory_space=pltpu.VMEM),) * 3,
        scratch_shapes=[pltpu.VMEM((WINDOW, QW), bf16)] * 2
        + [pltpu.VMEM((2 * WINDOW, HEAD), bf16)] * 2
        + [pltpu.VMEM((2 * WINDOW, HEAD), f32)] * 2
        + [pltpu.VMEM((WINDOW, QW), bf16)]
        + [pltpu.VMEM((WINDOW, HEAD), bf16)] * 6
        + [dma((4, WB))] * 2
        + [dma((2, WB))] * 4
        + [dma((WB,))] * 2
        + [dma((2, WB))] * 2,
        compiler_params=pltpu.CompilerParams(collective_id=0, has_side_effects=True),
        name="window_attention",
    )(docs, band, queries, keys, values, upstream)


def settle_kernel(*refs):
    ins, outs, sems = refs[:3], refs[3:6], refs[6]
    copies = [pltpu.make_async_copy(a, b, sems.at[n]) for n, (a, b) in enumerate(zip(ins, outs))]
    for copy in copies:
        copy.start()
    for copy in copies:
        copy.wait()


def settle(*grads):
    return pl.pallas_call(
        settle_kernel,
        out_shape=tuple(jax.ShapeDtypeStruct(a.shape, a.dtype) for a in grads),
        in_specs=[pl.BlockSpec(memory_space=pltpu.VMEM)] * 3,
        out_specs=(pl.BlockSpec(memory_space=pl.ANY),) * 3,
        scratch_shapes=[pltpu.SemaphoreType.DMA((3,))],
        name="settle",
    )(*(pltpu.with_memory_space_constraint(a, pltpu.VMEM) for a in grads))


def solution(mesh):
    cores = mesh.shape["heads"]
    planes = mesh.shape["blk"] * cores // WB

    def per_device(queries, keys, values, upstream, doc_ids, band):
        grads = window_attention(cores, planes, doc_ids, band, queries, keys, values, upstream)
        return settle(*grads)

    split = P(("groups", "blk", "heads"), None)
    return jax.shard_map(
        per_device,
        mesh=mesh,
        in_specs=(split,) * 4 + (P("groups"),) * 2,
        out_specs=(split,) * 3,
        check_vma=False,
    )
```

```python
import functools
import math

import jax
import jax.numpy as jnp
from jax import lax
from jax.experimental import pallas as pl
from jax.experimental.pallas import tpu as pltpu
from jax.sharding import PartitionSpec as P

HEAD = 128
SCALE = 168 ** -0.5
LOG2E = math.log2(math.e)
WINDOW = 1024
BLOCK = 128
WB = WINDOW // BLOCK
GROUP = 2
QW = GROUP * HEAD
MESH = pl.DeviceIdType.MESH
HIDDEN = -1e30
SPAN = WINDOW + BLOCK
NT = (((1,), (1,)), ((), ()))
TN = (((0,), (0,)), ((), ()))


def place(cores):
    chips = WB // cores
    blk, core = lax.axis_index("blk"), lax.axis_index("heads")
    return blk // chips, (blk % chips) * cores + core


def device_of(cores, plane, local):
    return {"blk": plane * (WB // cores) + local // cores, "heads": local % cores}


def greet(cores, planes, plane, me):
    barrier = pltpu.get_barrier_semaphore()

    def signal(where):
        pl.semaphore_signal(barrier, inc=1, device_id=where, device_id_type=MESH)

    for r in range(1, WB):
        signal(device_of(cores, plane, (me + r) % WB))

    @pl.when(plane > 0)
    def _():
        signal(device_of(cores, plane - 1, me))

    @pl.when(plane < planes - 1)
    def _():
        signal(device_of(cores, plane + 1, me))

    peers = WB - 1 + jnp.minimum(plane, 1) + jnp.minimum(planes - 1 - plane, 1)
    pl.semaphore_wait(barrier, peers)


def cols(index, width):
    return pl.ds(pl.multiple_of(index * width, width), width)


def rows(index, base=0):
    return pl.ds(pl.multiple_of(base + index * BLOCK, BLOCK), BLOCK)


def stack(x):
    return jnp.concatenate([x[:, :HEAD], x[:, HEAD:]], axis=0)


def score_terms(q, g, kb, vb):
    s = lax.dot_general(kb, q, NT, preferred_element_type=jnp.float32)
    dp = lax.dot_general(vb, g, NT, preferred_element_type=jnp.float32)
    return s, dp


def soft_terms(s, dp, seen):
    tiles = []
    for i in range(WB + 1):
        tile = s[i * BLOCK : (i + 1) * BLOCK]
        if i < WB:
            tile = jnp.where(WB + 1 - i <= seen, tile, HIDDEN)
        else:
            kpos = lax.broadcasted_iota(jnp.int32, tile.shape, 0)
            qpos = lax.broadcasted_iota(jnp.int32, tile.shape, 1) % BLOCK
            tile = jnp.where(kpos <= qpos, tile, HIDDEN)
        tiles.append(tile)
    s = jnp.concatenate(tiles, axis=0)
    top = jnp.max(s, axis=0, keepdims=True)
    e = jnp.exp2((s - top) * (SCALE * LOG2E))
    inverse = 1.0 / jnp.sum(e, axis=0, keepdims=True)
    delta = jnp.sum(e * dp, axis=0, keepdims=True) * inverse
    p = e * inverse
    return p.astype(jnp.bfloat16), (p * (dp - delta)).astype(jnp.bfloat16)


def grad_terms(pb, ds, q, g, kb):
    dv = jnp.dot(pb, g, preferred_element_type=jnp.float32)
    dk = jnp.dot(ds, q, preferred_element_type=jnp.float32)
    dq = lax.dot_general(kb, ds, TN, preferred_element_type=jnp.float32)
    dq = (dq * SCALE).T.astype(jnp.bfloat16)
    return jnp.concatenate([dq[:BLOCK], dq[BLOCK:]], axis=1), dk, dv


def window_kernel(
    cores, planes, docs, band, q, k, v, g, oq, ok, ov,
    qh, gh, kw, vw, dk, dv, dq, part_k, part_v, back_k, back_v, sum_k, sum_v,
    gsend, grecv, zsend, zrecv, bsend, brecv, qsend, qrecv, rsend, rrecv,
):
    plane, me = place(cores)
    first, last = plane == 0, plane == planes - 1
    sources = ((k, kw, HEAD, WINDOW), (v, vw, HEAD, WINDOW), (q, qh, QW, 0), (g, gh, QW, 0))
    partial = ((dk, part_k, back_k, sum_k, ok), (dv, part_v, back_v, sum_v, ov))

    def remote(src, dst, send, recv, where):
        return pltpu.make_async_remote_copy(
            src_ref=src, dst_ref=dst, send_sem=send, recv_sem=recv,
            device_id=where, device_id_type=MESH,
        )

    def landed(ref, sem):
        pltpu.make_async_copy(ref, ref, sem).wait()

    def exchange(n, to):
        src, dst, w, base = sources[n]
        return remote(
            src.at[:, cols(to, w)], dst.at[rows(me, base), :], gsend.at[n, to], grecv.at[n, me],
            device_of(cores, plane, to),
        )

    def forward(n, of):
        dst = sources[n][1]
        return remote(
            dst.at[rows(of, WINDOW), :], dst.at[rows(of), :], zsend.at[n, of], zrecv.at[n, of],
            device_of(cores, plane + 1, me),
        )

    def backward(n, of):
        _, part, back, _, _ = partial[n]
        return remote(
            part.at[rows(of), :], back.at[rows(of), :], bsend.at[n, of], brecv.at[n, of],
            device_of(cores, plane - 1, me),
        )

    def give(src, out, w, to, send, recv):
        source, target = src.at[rows(to), :], out.at[:, cols(me, w)]

        @pl.when(to != me)
        def _():
            remote(source, target, send, recv, device_of(cores, plane, to)).start()

        @pl.when(to == me)
        def _():
            pltpu.make_async_copy(source, target, recv).start()

    for n, (src, dst, w, base) in enumerate(sources):
        own = pltpu.make_async_copy(src.at[:, cols(me, w)], dst.at[rows(me, base), :], grecv.at[n, me])
        own.start()
    greet(cores, planes, plane, me)
    chip, core = me // 2, me % 2
    wide, tall, far = chip + 1 - 2 * (chip % 2), (chip + 2) % 4, 3 - chip
    x0, x1 = 2 * wide + core, 2 * wide + 1 - core
    y0, y1 = 2 * tall + core, 2 * tall + 1 - core
    d0, d1 = 2 * far + core, 2 * far + 1 - core
    beside = 2 * chip + 1 - core
    for to in (beside, x0, y0, x1, y1, d0, d1):
        for n in (0, 1):
            exchange(n, to).start()
    for to in (beside, y0, x0, y1, x1, d0, d1):
        for n in (2, 3):
            exchange(n, to).start()

    dk[...] = jnp.zeros_like(dk)
    dv[...] = jnp.zeros_like(dv)

    @pl.when(first)
    def _():
        kw[pl.ds(0, WINDOW), :] = jnp.zeros((WINDOW, HEAD), kw.dtype)
        vw[pl.ds(0, WINDOW), :] = jnp.zeros((WINDOW, HEAD), vw.dtype)

    for of in (me, beside, x0, y0, x1, y1, d0, d1):
        for n in (0, 1):
            landed(sources[n][1].at[rows(of, WINDOW), :], grecv.at[n, of])

            @pl.when(jnp.logical_not(last))
            def _():
                forward(n, of).start()

    @pl.when(jnp.logical_not(first))
    def _():
        for n in (0, 1):

            @pl.loop(0, WB)
            def _(of):
                landed(sources[n][1].at[rows(of), :], zrecv.at[n, of])

    def send_back(j):
        @pl.when(jnp.logical_not(first))
        def _():
            part_k[rows(j), :] = (dk[rows(j), :] * SCALE).astype(jnp.bfloat16)
            part_v[rows(j), :] = dv[rows(j), :].astype(jnp.bfloat16)
            backward(0, j).start()
            backward(1, j).start()

    def seen_by(t):
        block = plane * WB + t
        seen = jnp.int32(0)
        for d in range(WB + 1):
            at = jnp.maximum(block - d, 0)
            visible = (d <= band[block]) & (block >= d) & (docs[at] == docs[block])
            seen = seen + visible.astype(jnp.int32)
        return seen

    def load(t):
        span = pl.ds(pl.multiple_of(t * BLOCK, BLOCK), SPAN)
        return stack(qh[rows(t), :]), stack(gh[rows(t), :]), kw[span, :], vw[span, :]

    def store(t, out, key_term, value_term):
        span = pl.ds(pl.multiple_of(t * BLOCK, BLOCK), SPAN)
        dk[span, :] += key_term
        dv[span, :] += value_term
        dq[rows(t), :] = out

    upper = chip // 2
    near_first = (chip, 1 - chip, chip + 2, 3 - chip)
    own_first = (chip, chip - 2, 3 - chip, 5 - chip)
    order = [a + upper * (b - a) for a, b in zip(near_first, own_first)]

    def visit(i):
        return sum((i == n).astype(jnp.int32) * order[n] for n in range(4))

    due = []
    latest = jnp.int32(0)
    for p in range(4):
        when = sum(i * (order[i] == p).astype(jnp.int32) for i in range(4))
        latest = jnp.maximum(latest, when)
        due.append(latest)

    @pl.loop(0, WB // 2)
    def _(i):
        one = 2 * visit(i)
        two = one + 1
        for t in (one, two):
            landed(qh.at[rows(t), :], grecv.at[2, t])
            landed(gh.at[rows(t), :], grecv.at[3, t])
        seen_one, seen_two = seen_by(one), seen_by(two)
        q1, g1, k1, v1 = load(one)
        q2, g2, k2, v2 = load(two)
        s1, dp1 = score_terms(q1, g1, k1, v1)
        s2, dp2 = score_terms(q2, g2, k2, v2)
        pb1, ds1 = soft_terms(s1, dp1, seen_one)
        store(one, *grad_terms(pb1, ds1, q1, g1, k1))
        pb2, ds2 = soft_terms(s2, dp2, seen_two)
        store(two, *grad_terms(pb2, ds2, q2, g2, k2))

        for p in range(4):

            @pl.when(i == due[p])
            def _():
                send_back(jnp.int32(2 * p))
                send_back(jnp.int32(2 * p + 1))

        for t in (one, two):
            give(dq, oq, QW, t, qsend.at[t], qrecv.at[me])

    @pl.loop(0, WB)
    def _(j):
        for n in (0, 1):
            acc, _, back, total, out = partial[n]
            factor = SCALE if n == 0 else 1.0

            @pl.when(jnp.logical_not(last))
            def _():
                landed(back.at[rows(j), :], brecv.at[n, j])
                both = acc[rows(j, WINDOW), :] * factor + back[rows(j), :].astype(jnp.float32)
                total[rows(j), :] = both.astype(jnp.bfloat16)

            @pl.when(last)
            def _():
                total[rows(j), :] = (acc[rows(j, WINDOW), :] * factor).astype(jnp.bfloat16)

        for n in (0, 1):
            _, _, _, total, out = partial[n]
            give(total, out, HEAD, j, rsend.at[n, j], rrecv.at[n, me])

    @pl.loop(0, WB)
    def _(s):
        landed(oq.at[:, cols(s, QW)], qrecv.at[s])
        landed(ok.at[:, cols(s, HEAD)], rrecv.at[0, s])
        landed(ov.at[:, cols(s, HEAD)], rrecv.at[1, s])

        @pl.when(s != me)
        def _():
            for n in range(4):
                exchange(n, s).wait_send()
            where = device_of(cores, plane, s)
            remote(dq.at[rows(s), :], oq.at[:, cols(me, QW)], qsend.at[s], qrecv.at[me], where).wait_send()
            for n in (0, 1):
                _, _, _, total, out = partial[n]
                remote(
                    total.at[rows(s), :], out.at[:, cols(me, HEAD)], rsend.at[n, s], rrecv.at[n, me], where
                ).wait_send()

        for n in (0, 1):

            @pl.when(jnp.logical_not(last))
            def _():
                forward(n, s).wait_send()

            @pl.when(jnp.logical_not(first))
            def _():
                backward(n, s).wait_send()


def window_attention(cores, planes, docs, band, queries, keys, values, upstream):
    hbm = pl.BlockSpec(memory_space=pl.ANY)
    smem = pl.BlockSpec(memory_space=pltpu.SMEM)
    bf16, f32 = jnp.bfloat16, jnp.float32
    dma = pltpu.SemaphoreType.DMA
    return pl.pallas_call(
        functools.partial(window_kernel, cores, planes),
        out_shape=tuple(pltpu.VMEM(a.shape, bf16) for a in (queries, keys, values)),
        in_specs=[smem] * 2 + [hbm] * 4,
        out_specs=(pl.BlockSpec(memory_space=pltpu.VMEM),) * 3,
        scratch_shapes=[pltpu.VMEM((WINDOW, QW), bf16)] * 2
        + [pltpu.VMEM((2 * WINDOW, HEAD), bf16)] * 2
        + [pltpu.VMEM((2 * WINDOW, HEAD), f32)] * 2
        + [pltpu.VMEM((WINDOW, QW), bf16)]
        + [pltpu.VMEM((WINDOW, HEAD), bf16)] * 6
        + [dma((4, WB))] * 2
        + [dma((2, WB))] * 4
        + [dma((WB,))] * 2
        + [dma((2, WB))] * 2,
        compiler_params=pltpu.CompilerParams(collective_id=0, has_side_effects=True),
        name="window_attention",
    )(docs, band, queries, keys, values, upstream)


def settle_kernel(*refs):
    ins, outs, sems = refs[:3], refs[3:6], refs[6]
    copies = [pltpu.make_async_copy(a, b, sems.at[n]) for n, (a, b) in enumerate(zip(ins, outs))]
    for copy in copies:
        copy.start()
    for copy in copies:
        copy.wait()


def settle(*grads):
    return pl.pallas_call(
        settle_kernel,
        out_shape=tuple(jax.ShapeDtypeStruct(a.shape, a.dtype) for a in grads),
        in_specs=[pl.BlockSpec(memory_space=pltpu.VMEM)] * 3,
        out_specs=(pl.BlockSpec(memory_space=pl.ANY),) * 3,
        scratch_shapes=[pltpu.SemaphoreType.DMA((3,))],
        name="settle",
    )(*(pltpu.with_memory_space_constraint(a, pltpu.VMEM) for a in grads))


def solution(mesh):
    cores = mesh.shape["heads"]
    planes = mesh.shape["blk"] * cores // WB

    def per_device(queries, keys, values, upstream, doc_ids, band):
        grads = window_attention(cores, planes, doc_ids, band, queries, keys, values, upstream)
        return settle(*grads)

    split = P(("groups", "blk", "heads"), None)
    return jax.shard_map(
        per_device,
        mesh=mesh,
        in_specs=(split,) * 4 + (P("groups"),) * 2,
        out_specs=(split,) * 3,
        check_vma=False,
    )
```
